32 devices in a mesh: region: 4 (over z), enc: 8 (over y, x, core).
Axes of the slice: x: 2, y: 2, z: 4, core: 2. Of those that a mesh axis runs over, the one named last changes fastest.
Arguments:
- pixels: bfloat16 [256, 48, 4096], P(('region', 'enc')), may hold values from -6 to 6
- feature_grad: bfloat16 [256, 96, 4096], P(('region', 'enc')), may hold values from -0.0046691895 to 0.0046691895
- tissue_count: int32 [32], P(('region', 'enc')), may hold values from 1 to 8, as said below
- stem_weight: bfloat16 [96, 48], replicated, may hold values from -0.875 to 0.875
- stem_gain: float32 [96], replicated, may hold values from 0.5 to 1.5
- stem_shift: float32 [96], replicated, may hold values from -3 to 3
- depth_kernel: float32 [96, 49], replicated, may hold values from -0.875 to 0.875
- block_gain: float32 [96], replicated, may hold values from 0.5 to 1.5
- expand_weight: bfloat16 [384, 96], replicated, may hold values from -0.625 to 0.625
- expand_bias: float32 [384], replicated, may hold values from -3 to 3
- reduce_weight: bfloat16 [96, 384], replicated, may hold values from -0.3125 to 0.3125
- layer_scale: float32 [96], replicated, may hold values from 0.5 to 1.5
Outputs:
- features: bfloat16 [256, 96, 4096], P(('region', 'enc'))
- grad_stem: float32 [96, 48], replicated
- grad_gain: float32 [96], replicated
- grad_shift: float32 [96], replicated
- grad_kernel: float32 [96, 49], replicated
- grad_norm: float32 [96], replicated
- grad_expand: float32 [384, 96], replicated
- grad_bias: float32 [384], replicated
- grad_reduce: float32 [96, 384], replicated
- grad_scale: float32 [96], replicated
The draws below stay inside these ranges and needn't reach their ends.
Inputs may be any that keep to these rules, and one draw needn't show every extreme that they name: `tissue_count`: the tissue tiles of a device fill its first slots; the other slots are unused.
All inputs are finite; a program needn't handle non-finite values.
Results may differ from the reference program's by a relative error of at most 0.015.
Values may be sent and summed in bfloat16 or wider, within the bound.
A program may use at most 256 MiB of HBM per device.

```python
from functools import partial
import jax
import jax.numpy as jnp
from jax import lax

C = 96
HID = 384
PATCH = 48
SIDE = 64
KSIZE = 7
SLOTS = 8
TILES = 256
N_REGION = 4
N_ENC = 8


def draw_tissue_count(key, part):
    first, second, fourth = jax.random.split(key, 3)
    shape = (N_REGION * N_ENC,)
    lowest = jnp.minimum(jax.random.randint(first, shape, 1, SLOTS + 1), jax.random.randint(second, shape, 1, SLOTS + 1))
    picked = jax.random.randint(fourth, (N_REGION,), 0, N_ENC)
    device_index = jnp.arange(N_REGION * N_ENC, dtype=jnp.int32)
    filled = device_index % N_ENC == picked[device_index // N_ENC]
    return jnp.where(filled, SLOTS, lowest).astype(jnp.int32)


def steps_of(rng, dims, shards, smallest, largest):
    def one(axis_at, shards_of):
        steps = jax.random.uniform(jax.random.fold_in(jax.random.fold_in(rng, 6), axis_at), (shards_of,), jnp.float32, smallest / len(shards), largest / len(shards))
        return jnp.repeat(jnp.exp(steps), dims[axis_at] // shards_of).reshape((-1,) + (1,) * (len(dims) - axis_at - 1))

    factor_of = one(*shards[0])
    for cut in shards[1:]:
        factor_of = factor_of * one(*cut)
    return factor_of


def gaussian(key, dims, scale, bound, pieces=(), kind=jnp.bfloat16):
    gain = steps_of(key, dims, pieces, -0.22, 0.18) if pieces else 1.0
    values = jax.random.normal(key, dims, jnp.float32) * scale * gain
    return jnp.minimum(jnp.maximum(values, -bound), bound).astype(kind)


def setup_inputs(seed: int = 0) -> dict:
    arg_keys = jax.random.split(jax.random.key(seed), 13)
    return {
        "pixels": gaussian(arg_keys[0], (TILES, PATCH, SIDE * SIDE), 1.0, 6.0, ((0, 32),)),
        "feature_grad": gaussian(arg_keys[1], (TILES, C, SIDE * SIDE), (0.05 / SIDE), 0.0046691895, ((0, 32),)),
        "tissue_count": draw_tissue_count(jax.random.fold_in(arg_keys[12], 71), 0),
        "stem_weight": gaussian(arg_keys[3], (C, PATCH), PATCH ** -0.5, 0.875),
        "stem_gain": jnp.clip(1.0 + 0.1 * jax.random.normal(arg_keys[4], (C,), jnp.float32), 0.5, 1.5),
        "stem_shift": gaussian(arg_keys[5], (C,), 0.5, 3.0, (), jnp.float32),
        "depth_kernel": gaussian(arg_keys[6], (C, KSIZE * KSIZE), (KSIZE * KSIZE) ** -0.5, 0.875, (), jnp.float32),
        "block_gain": jnp.clip(1.0 + 0.1 * jax.random.normal(arg_keys[7], (C,), jnp.float32), 0.5, 1.5),
        "expand_weight": gaussian(arg_keys[8], (HID, C), C ** -0.5, 0.625),
        "expand_bias": gaussian(arg_keys[9], (HID,), 0.5, 3.0, (), jnp.float32),
        "reduce_weight": gaussian(arg_keys[10], (C, HID), HID ** -0.5, 0.3125),
        "layer_scale": jnp.clip(jax.random.uniform(arg_keys[11], (C,), jnp.float32, 0.5, 1.5), 0.5, 1.5),
    }


EPS = 1e-06

def channel_norm(values, channel_gain, channel_shift):
    centre = lax.optimization_barrier(jnp.mean(values, axis=0, keepdims=True))
    spread = lax.optimization_barrier(jnp.mean(jnp.square(values - centre), axis=0, keepdims=True))
    return (values - centre) * lax.rsqrt(spread + EPS) * channel_gain[:, None] + channel_shift[:, None]

def depthwise(values, kernel):
    margin = 3 * SIDE + 3
    padded = jnp.pad(values, ((0, 0), (margin, margin)))
    column = jnp.arange(SIDE * SIDE, dtype=jnp.int32) % SIDE
    result = jnp.zeros_like(values)
    for row_step in range(-3, 4):
        for col_step in range(-3, 4):
            offset = margin + row_step * SIDE + col_step
            shifted = padded[:, offset:offset + SIDE * SIDE]
            inside = (column + col_step >= 0) & (column + col_step < SIDE)
            weight = kernel[:, (row_step + 3) * KSIZE + col_step + 3]
            result = result + weight[:, None] * jnp.where(inside[None, :], shifted, jnp.zeros_like(shifted))
    return result

def forward(weights, tile_pixels):
    stem_weight, stem_gain, stem_shift, depth_kernel, block_gain, expand_weight, expand_bias, reduce_weight, layer_scale = weights
    stem_out = jnp.dot(stem_weight.astype(jnp.bfloat16), tile_pixels, preferred_element_type=jnp.float32)
    base = lax.optimization_barrier(channel_norm(stem_out, stem_gain, stem_shift).astype(jnp.bfloat16))
    mixed = depthwise(base.astype(jnp.float32), depth_kernel)
    normed = channel_norm(mixed, block_gain, jnp.zeros_like(block_gain)).astype(jnp.bfloat16)
    expand = jnp.dot(expand_weight.astype(jnp.bfloat16), normed, preferred_element_type=jnp.float32) + expand_bias[:, None]
    hidden = jax.nn.gelu(expand, approximate=False).astype(jnp.bfloat16)
    reduced = jnp.dot(reduce_weight.astype(jnp.bfloat16), hidden, preferred_element_type=jnp.float32)
    return (base.astype(jnp.float32) + layer_scale[:, None] * reduced).astype(jnp.bfloat16)

def encode(weights, tile_pixels, tile_grad):
    block_out, pullback = jax.vjp(partial(forward, tile_pixels=tile_pixels), weights)
    return (block_out, pullback(tile_grad)[0])

def reference(pixels, feature_grad, tissue_count, stem_weight, stem_gain, stem_shift, depth_kernel, block_gain, expand_weight, expand_bias, reduce_weight, layer_scale):
    weights = tuple((member.astype(jnp.float32) for member in (stem_weight, stem_gain, stem_shift, depth_kernel, block_gain, expand_weight, expand_bias, reduce_weight, layer_scale)))
    slot_index = jnp.arange(pixels.shape[0], dtype=jnp.int32)
    live = slot_index % SLOTS < tissue_count[slot_index // SLOTS]
    zero_grads = jax.tree.map(jnp.zeros_like, weights)

    def scan_step(totals, inputs):
        tile_pixels, tile_grad, occupied = inputs

        def compute(operand):
            return encode(weights, tile_pixels, tile_grad)

        def skipped(operand):
            return (jnp.zeros(tile_grad.shape, tile_grad.dtype), zero_grads)
        block_out, grads = lax.cond(occupied, compute, skipped, 0)
        return (jax.tree.map(jnp.add, totals, grads), block_out)
    totals, features = lax.scan(scan_step, zero_grads, (pixels, feature_grad, live))
    return (features, totals[0], totals[1], totals[2], totals[3], totals[4], totals[5], totals[6], totals[7], totals[8])
```

```python
from functools import partial

import jax
import jax.numpy as jnp
import numpy as np
from jax import lax
from jax.experimental import pallas as pl
from jax.experimental.pallas import tpu as pltpu
from jax.sharding import PartitionSpec as P

SIDE = 64
KSIZE = 7
EPS = 1e-06
LANES = 128
CHUNK = 512
PAD = 2
BLOCKS = 10
EXTRA = 16

f32 = jnp.float32
bf16 = jnp.bfloat16


def dot(a, b, dims=((1,), (0,))):
    return lax.dot_general(a, b, (dims, ((), ())), preferred_element_type=f32)


def wide(value, times):
    return jnp.concatenate([value] * times, axis=1)


def fold(value):
    total = value[:, :LANES]
    for at in range(LANES, value.shape[1], LANES):
        total = total + value[:, at : at + LANES]
    return total


def unit(values):
    centre = jnp.mean(values, axis=0, keepdims=True)
    shifted = values - centre
    spread = jnp.mean(jnp.square(shifted), axis=0, keepdims=True)
    scale = lax.rsqrt(spread + EPS)
    return shifted * scale, scale


def unit_back(grad, hat, scale):
    first = jnp.mean(grad, axis=0, keepdims=True)
    second = jnp.mean(grad * hat, axis=0, keepdims=True)
    return scale * (grad - first - hat * second)


def gelu_both(x):
    decay = jnp.exp(x * x * -0.5)
    t = 1.0 / (1.0 + jnp.abs(x) * (0.3275911 * 0.7071067811865476))
    poly = t * (
        0.5 * 0.254829592
        + t
        * (
            0.5 * -0.284496736
            + t * (0.5 * 1.421413741 + t * (0.5 * -1.453152027 + t * (0.5 * 1.061405429)))
        )
    )
    tail = poly * decay
    cdf = jnp.where(x >= 0, 1.0 - tail, tail)
    return x * cdf, cdf + x * (decay * 0.3989422804014327)


def body(
    count_ref, pix_ref, grad_ref, ws_ref, par_ref, we_ref, wet_ref, wr_ref, wrt_ref, taps_ref,
    back_ref, feat_ref, dws_ref, dvec_ref, dwe_ref, dwr_ref, dk_ref, base_s, mix_s, ex_s, dh_s,
    hid_s, de_s,
):
    phase = pl.program_id(0)
    slot = pl.program_id(1)
    slots = pl.num_programs(1)
    live = slot < count_ref[0]
    channels, area = grad_ref.shape[1:]
    pairs = area // LANES
    per = CHUNK // LANES
    chunks = area // CHUNK
    hidden = we_ref.shape[0]
    rows = base_s.shape[1] // channels

    row_at = lax.broadcasted_iota(jnp.int32, (SIDE, LANES), 0)
    lane_at = lax.broadcasted_iota(jnp.int32, (SIDE, LANES), 1) % SIDE
    near = jnp.abs(row_at - lane_at) <= KSIZE // 2
    near_mirrored = jnp.abs(SIDE - 1 - row_at - lane_at) <= KSIZE // 2
    row_all = lax.broadcasted_iota(jnp.int32, (LANES, LANES), 0)
    lane_all = lax.broadcasted_iota(jnp.int32, (LANES, LANES), 1)
    same = row_all // SIDE == lane_all // SIDE
    mirror = (same & (row_all % SIDE + lane_all % SIDE == SIDE - 1)).astype(f32).astype(bf16)

    def read(ref, chunk):
        return jnp.concatenate(
            [
                ref[PAD + chunk * per + at, pl.ds(slot, channels, stride=rows), :]
                for at in range(per)
            ],
            axis=1,
        )

    def write(ref, chunk, value):
        for at in range(per):
            ref[PAD + chunk * per + at, pl.ds(slot, channels, stride=rows), :] = value[
                :, at * LANES : (at + 1) * LANES
            ]

    def param(at):
        return wide(par_ref[at], per)

    def toeplitz(ref, c):
        blocks = []
        for m in range(BLOCKS):
            row = jnp.broadcast_to(ref[c, m : m + 1, :], (SIDE, LANES))
            turned = pltpu.roll(row, 0, 1, stride=1, stride_axis=0)
            blocks.append(jnp.where(near, turned, 0.0).astype(bf16))
        return jnp.concatenate(blocks, axis=0)

    def gathered(ref, c):
        at = pl.multiple_of(c * rows, rows)
        full = ref[:, pl.ds(at, rows), :]
        even = full.reshape((pairs + 2 * PAD) * rows, LANES).astype(bf16)
        odd = full[1 : pairs + 3].reshape((pairs + 2) * rows, LANES).astype(bf16)
        size = pairs * rows
        return jnp.concatenate(
            [
                even[:size],
                odd[:size],
                even[2 * rows : 2 * rows + size],
                odd[2 * rows : 2 * rows + size],
                even[4 * rows : 4 * rows + size],
            ],
            axis=1,
        )

    @pl.when((phase == 0) & (slot == 0))
    def _():
        base_s[...] = jnp.zeros(base_s.shape, f32)
        mix_s[...] = jnp.zeros(mix_s.shape, f32)
        dws_ref[...] = jnp.zeros(dws_ref.shape, f32)
        dvec_ref[...] = jnp.zeros(dvec_ref.shape, f32)
        dwe_ref[...] = jnp.zeros(dwe_ref.shape, f32)
        dwr_ref[...] = jnp.zeros(dwr_ref.shape, f32)

    @pl.when((phase == 0) & live)
    def _():
        @pl.loop(0, chunks)
        def _(chunk):
            at = pl.multiple_of(chunk * CHUNK, CHUNK)
            out = dot(ws_ref[...], pix_ref[0, :, pl.ds(at, CHUNK)])
            hat, _ = unit(out)
            base = (hat * param(0) + param(1)).astype(bf16).astype(f32)
            write(base_s, chunk, base)

    @pl.when((phase == 1) & (slot == 0))
    def _():
        @pl.loop(0, channels)
        def _(c):
            out = dot(gathered(base_s, c), toeplitz(taps_ref, c))
            at = pl.multiple_of(c * rows, rows)
            mix_s[PAD : PAD + pairs, pl.ds(at, rows), :] = out.reshape(pairs, rows, LANES)

    @pl.when((phase == 1) & live)
    def _():
        @pl.loop(0, chunks)
        def _(chunk):
            at = pl.multiple_of(chunk * CHUNK, CHUNK)
            hat, scale = unit(read(mix_s, chunk))
            normed = (hat * param(2)).astype(bf16)
            normed = jnp.concatenate([normed, jnp.ones((EXTRA, CHUNK), bf16)], axis=0)
            grad = grad_ref[0, :, pl.ds(at, CHUNK)]
            ex_s[...] = dot(we_ref[...], normed)
            dh_s[...] = dot(wrt_ref[...], (grad.astype(f32) * param(3)).astype(bf16))
            for h in range(0, hidden, 16):
                act, slope = gelu_both(ex_s[h : h + 16, :])
                hid_s[h : h + 16, :] = act.astype(bf16)
                de_s[h : h + 16, :] = (slope * dh_s[h : h + 16, :]).astype(bf16)
            reduced = dot(wr_ref[...], hid_s[...])
            feat_ref[0, :, pl.ds(at, CHUNK)] = (
                read(base_s, chunk) + param(3) * reduced
            ).astype(bf16)
            dwr_ref[...] += dot(grad, hid_s[...], ((1,), (1,)))
            dwe_ref[...] += dot(de_s[...], normed, ((1,), (1,)))
            dn = dot(wet_ref[...], de_s[...])
            dvec_ref[2] += fold(dn * hat)
            write(mix_s, chunk, unit_back(dn * param(2), hat, scale))

    @pl.when((phase == 1) & jnp.logical_not(live))
    def _():
        feat_ref[...] = jnp.zeros(feat_ref.shape, bf16)

    @pl.when((phase == 2) & (slot == 0))
    def _():
        @pl.loop(0, channels)
        def _(c):
            at = pl.multiple_of(c * rows, rows)
            grad = mix_s[PAD : PAD + pairs, pl.ds(at, rows), :]
            grad = grad.reshape(pairs * rows, LANES).astype(bf16)
            grad = dot(grad, mirror).astype(bf16)
            cross = dot(grad, gathered(base_s, c), ((0,), (0,)))
            for r in range(2):
                for k in range(BLOCKS // 2):
                    part = cross[r * SIDE : (r + 1) * SIDE, k * LANES : (k + 1) * LANES]
                    part = pltpu.roll(
                        jnp.where(near_mirrored, part, 0.0), 0, 1, stride=1, stride_axis=0
                    )
                    dk_ref[c, r * 5 + k : r * 5 + k + 1, :] = jnp.sum(
                        part, axis=0, keepdims=True
                    )
            out = dot(gathered(mix_s, c), toeplitz(back_ref, c))
            mix_s[PAD : PAD + pairs, pl.ds(at, rows), :] = out.reshape(pairs, rows, LANES)

    @pl.when((phase == 2) & live)
    def _():
        @pl.loop(0, chunks)
        def _(chunk):
            at = pl.multiple_of(chunk * CHUNK, CHUNK)
            pix = pix_ref[0, :, pl.ds(at, CHUNK)]
            hat, scale = unit(dot(ws_ref[...], pix))
            dbase = grad_ref[0, :, pl.ds(at, CHUNK)].astype(f32) + read(mix_s, chunk)
            dvec_ref[0] += fold(dbase * hat)
            dvec_ref[1] += fold(dbase)
            dstem = unit_back(dbase * param(0), hat, scale).astype(bf16)
            dws_ref[...] += dot(dstem, pix, ((1,), (1,)))


def tap_places():
    half = KSIZE // 2
    place = np.zeros((KSIZE * KSIZE, 16, LANES), np.float32)
    pick = np.zeros((BLOCKS, LANES, KSIZE * KSIZE), np.float32)
    for m in range(BLOCKS):
        for r in range(2):
            a = m - 2 * PAD - r
            if abs(a) > half:
                continue
            for b in range(-half, half + 1):
                tap = (a + half) * KSIZE + b + half
                place[tap, m, (r * SIDE - b) % LANES] = 1.0
                k, rr = divmod(m, 2)
                pick[r * 5 + k, (rr * SIDE + b + SIDE - 1) % LANES, tap] = 1.0
    return place.reshape(KSIZE * KSIZE, -1), pick.reshape(-1, KSIZE * KSIZE)


def encode_slots(pixels, feature_grad, count, weights):
    (ws, stem_gain, stem_shift, kernel, block_gain, we, bias, wr, layer_scale) = weights
    slots, patch, area = pixels.shape
    channels = ws.shape[0]
    hidden = we.shape[0]
    pairs = area // LANES
    place, pick = tap_places()
    exact = lax.Precision.HIGHEST
    taps = jnp.dot(kernel, place, precision=exact).reshape(channels, 16, LANES)
    back = jnp.dot(kernel[:, ::-1], place, precision=exact).reshape(channels, 16, LANES)
    params = jnp.stack([stem_gain, stem_shift, block_gain, layer_scale])
    params = jnp.broadcast_to(params[:, :, None], (4, channels, LANES))
    high = lax.reduce_precision(bias, 8, 7)
    middle = lax.reduce_precision(bias - high, 8, 7)
    low = bias - high - middle
    extra = jnp.stack([high, middle, low], axis=1).astype(bf16)
    we_all = jnp.concatenate(
        [we, extra, jnp.zeros((hidden, EXTRA - extra.shape[1]), bf16)], axis=1
    )

    def pix_at(phase, slot, count):
        last = count[0] - 1
        return (jnp.where(phase == 1, last, jnp.minimum(slot, last)), 0, 0)

    def grad_at(phase, slot, count):
        return (jnp.where(phase == 0, 0, jnp.minimum(slot, count[0] - 1)), 0, 0)

    def feat_at(phase, slot, count):
        return (jnp.where(phase == 0, 0, jnp.where(phase == 1, slot, slots - 1)), 0, 0)

    def whole(shape):
        return pl.BlockSpec(shape, lambda phase, slot, count: (0,) * len(shape))

    consts = (ws, params, we_all, we.T, wr, wr.T, taps, back)
    sums = [
        (channels, patch),
        (3, channels, LANES),
        (hidden, channels + EXTRA),
        (channels, hidden),
        (channels, 16, LANES),
    ]
    outs = pl.pallas_call(
        body,
        grid_spec=pltpu.PrefetchScalarGridSpec(
            num_scalar_prefetch=1,
            grid=(3, slots),
            in_specs=[
                pl.BlockSpec((1, patch, area), pix_at),
                pl.BlockSpec((1, channels, area), grad_at),
            ]
            + [whole(item.shape) for item in consts],
            out_specs=[pl.BlockSpec((1, channels, area), feat_at)] + [whole(s) for s in sums],
            scratch_shapes=[
                pltpu.VMEM((pairs + 2 * PAD, channels * slots, LANES), f32),
                pltpu.VMEM((pairs + 2 * PAD, channels * slots, LANES), f32),
                pltpu.VMEM((hidden, CHUNK), f32),
                pltpu.VMEM((hidden, CHUNK), f32),
                pltpu.VMEM((hidden, CHUNK), bf16),
                pltpu.VMEM((hidden, CHUNK), bf16),
            ],
        ),
        out_shape=[jax.ShapeDtypeStruct((slots, channels, area), bf16)]
        + [jax.ShapeDtypeStruct(s, f32) for s in sums],
        compiler_params=pltpu.CompilerParams(
            dimension_semantics=("arbitrary", "arbitrary"), vmem_limit_bytes=60 * 2**20
        ),
    )(count, pixels, feature_grad, *consts)
    features, dws, dvec, dwe, dwr, dk = outs
    dvec = jnp.sum(dvec, axis=2)
    dk = jnp.dot(dk[:, :BLOCKS].reshape(channels, -1), pick, precision=exact)
    totals = (
        dws,
        dvec[0],
        dvec[1],
        dk,
        dvec[2],
        dwe[:, :channels],
        dwe[:, channels],
        dwr * layer_scale[:, None],
        jnp.sum(dwr * wr.astype(f32), axis=1),
    )
    return features, totals


def on_device(pixels, feature_grad, tissue_count, *weights):
    features, totals = encode_slots(pixels, feature_grad, tissue_count, weights)
    shapes = [item.shape for item in totals]
    flat = jnp.concatenate([item.reshape(-1) for item in totals])
    flat = lax.psum(flat, ("region", "enc"))
    summed = []
    at = 0
    for shape in shapes:
        size = int(np.prod(shape))
        summed.append(flat[at : at + size].reshape(shape))
        at += size
    return (features, *summed)


def solution(mesh):
    return jax.shard_map(
        on_device,
        mesh=mesh,
        in_specs=(
            P(("region", "enc"), None, None),
            P(("region", "enc"), None, None),
            P(("region", "enc")),
        )
        + (P(),) * 9,
        out_specs=(P(("region", "enc"), None, None),) + (P(),) * 9,
        check_vma=False,
    )
```

```python
import jax
import jax.numpy as jnp
import numpy as np
from jax import lax
from jax.experimental import pallas as pl
from jax.experimental.pallas import tpu as pltpu
from jax.sharding import PartitionSpec as P

SIDE = 64
KSIZE = 7
EPS = 1e-06
LANES = 128
CHUNK = 512
PAD = 2
BLOCKS = 10
EXACT = lax.Precision.HIGHEST
MESH = pl.DeviceIdType.MESH

f32 = jnp.float32
bf16 = jnp.bfloat16


def dot(a, b, dims=((1,), (0,))):
    return lax.dot_general(a, b, (dims, ((), ())), preferred_element_type=f32)


def wide(value, times):
    return jnp.concatenate([value] * times, axis=1)


def fold(value):
    total = value[:, :LANES]
    for at in range(LANES, value.shape[1], LANES):
        total = total + value[:, at : at + LANES]
    return total


def unit(values):
    centre = jnp.mean(values, axis=0, keepdims=True)
    shifted = values - centre
    spread = jnp.mean(jnp.square(shifted), axis=0, keepdims=True)
    scale = lax.rsqrt(spread + EPS)
    return shifted * scale, scale


def unit_back(grad, hat, scale):
    first = jnp.mean(grad, axis=0, keepdims=True)
    second = jnp.mean(grad * hat, axis=0, keepdims=True)
    return scale * (grad - first - hat * second)


def gelu_both(x):
    decay = jnp.exp(x * x * -0.5)
    t = 1.0 / (1.0 + jnp.abs(x) * (0.3275911 * 0.7071067811865476))
    poly = t * (
        0.5 * 0.254829592
        + t
        * (
            0.5 * -0.284496736
            + t * (0.5 * 1.421413741 + t * (0.5 * -1.453152027 + t * (0.5 * 1.061405429)))
        )
    )
    tail = poly * decay
    cdf = jnp.where(x >= 0, 1.0 - tail, tail)
    return x * cdf, cdf + x * (decay * 0.3989422804014327)


def body(
    count_ref, pix_ref, grad_ref, ws_ref, gain_ref, shift_ref, norm_ref, scale_ref, kernel_ref,
    we_in_ref, bias_ref, wr_ref, place_ref, place_back_ref, pick_ref, feat_ref, sums_ref, base_s,
    mix_s, ex_s, dh_s, hid_s, de_s, par_ref, we_ref, wet_ref, wrt_ref, taps_ref, back_ref,
    dws_ref, dvec_ref, dwe_ref, dwr_ref, dk_ref,
):
    phase = pl.program_id(0)
    slot = pl.program_id(1)
    slots = pl.num_programs(1)
    live = slot < count_ref[0]
    channels, area = grad_ref.shape[1:]
    pairs = area // LANES
    per = CHUNK // LANES
    chunks = area // CHUNK
    hidden = we_ref.shape[0]
    rows = base_s.shape[1] // channels

    row_at = lax.broadcasted_iota(jnp.int32, (SIDE, LANES), 0)
    lane_at = lax.broadcasted_iota(jnp.int32, (SIDE, LANES), 1) % SIDE
    near = jnp.abs(row_at - lane_at) <= KSIZE // 2
    near_mirrored = jnp.abs(SIDE - 1 - row_at - lane_at) <= KSIZE // 2
    row_all = lax.broadcasted_iota(jnp.int32, (LANES, LANES), 0)
    lane_all = lax.broadcasted_iota(jnp.int32, (LANES, LANES), 1)
    same = row_all // SIDE == lane_all // SIDE
    mirror = (same & (row_all % SIDE + lane_all % SIDE == SIDE - 1)).astype(f32).astype(bf16)

    def read(ref, chunk):
        return jnp.concatenate(
            [
                ref[PAD + chunk * per + at, pl.ds(slot, channels, stride=rows), :]
                for at in range(per)
            ],
            axis=1,
        )

    def write(ref, chunk, value):
        for at in range(per):
            ref[PAD + chunk * per + at, pl.ds(slot, channels, stride=rows), :] = value[
                :, at * LANES : (at + 1) * LANES
            ]

    def param(at):
        return wide(par_ref[at], per)

    def toeplitz(ref, c):
        blocks = []
        for m in range(BLOCKS):
            row = jnp.broadcast_to(ref[c, m : m + 1, :], (SIDE, LANES))
            turned = pltpu.roll(row, 0, 1, stride=1, stride_axis=0)
            blocks.append(jnp.where(near, turned, 0.0).astype(bf16))
        return jnp.concatenate(blocks, axis=0)

    def gathered(ref, c):
        at = pl.multiple_of(c * rows, rows)
        full = ref[:, pl.ds(at, rows), :]
        even = full.reshape((pairs + 2 * PAD) * rows, LANES).astype(bf16)
        odd = full[1 : pairs + 3].reshape((pairs + 2) * rows, LANES).astype(bf16)
        size = pairs * rows
        return jnp.concatenate(
            [
                even[:size],
                odd[:size],
                even[2 * rows : 2 * rows + size],
                odd[2 * rows : 2 * rows + size],
                even[4 * rows : 4 * rows + size],
            ],
            axis=1,
        )

    @pl.when((phase == 0) & (slot == 0))
    def _():
        base_s[...] = jnp.zeros(base_s.shape, f32)
        mix_s[...] = jnp.zeros(mix_s.shape, f32)
        dws_ref[...] = jnp.zeros(dws_ref.shape, f32)
        dvec_ref[...] = jnp.zeros(dvec_ref.shape, f32)
        dwe_ref[...] = jnp.zeros(dwe_ref.shape, f32)
        dwr_ref[...] = jnp.zeros(dwr_ref.shape, f32)
        for at, ref in enumerate((gain_ref, shift_ref, norm_ref, scale_ref)):
            par_ref[at] = jnp.transpose(jnp.broadcast_to(ref[...], (LANES, channels)))
        kernel = kernel_ref[...].astype(bf16)
        for m in range(BLOCKS):
            taps_ref[:, m, :] = dot(kernel, place_ref[m])
            back_ref[:, m, :] = dot(kernel, place_back_ref[m])
        weight = we_in_ref[...].astype(f32)
        wet_ref[...] = jnp.transpose(weight).astype(bf16)
        wrt_ref[...] = jnp.transpose(wr_ref[...].astype(f32)).astype(bf16)
        bias = jnp.transpose(jnp.broadcast_to(bias_ref[...], (LANES, hidden)))
        high = bias.astype(bf16).astype(f32)
        middle = (bias - high).astype(bf16).astype(f32)
        low = bias - high - middle
        lane = lax.broadcasted_iota(jnp.int32, (hidden, LANES), 1)
        extra = jnp.where(
            lane == channels,
            high,
            jnp.where(lane == channels + 1, middle, jnp.where(lane == channels + 2, low, 0.0)),
        )
        we_ref[...] = extra.astype(bf16)
        we_ref[:, :channels] = we_in_ref[...]

    @pl.when((phase == 0) & live)
    def _():
        @pl.loop(0, chunks, unroll=2)
        def _(chunk):
            at = pl.multiple_of(chunk * CHUNK, CHUNK)
            out = dot(ws_ref[...], pix_ref[0, :, pl.ds(at, CHUNK)])
            hat, _ = unit(out)
            base = (hat * param(0) + param(1)).astype(bf16).astype(f32)
            write(base_s, chunk, base)

    @pl.when((phase == 1) & (slot == 0))
    def _():
        @pl.loop(0, channels, unroll=4)
        def _(c):
            out = dot(gathered(base_s, c), toeplitz(taps_ref, c))
            at = pl.multiple_of(c * rows, rows)
            mix_s[PAD : PAD + pairs, pl.ds(at, rows), :] = out.reshape(pairs, rows, LANES)

    @pl.when((phase == 1) & live)
    def _():
        @pl.loop(0, chunks, unroll=2)
        def _(chunk):
            at = pl.multiple_of(chunk * CHUNK, CHUNK)
            hat, scale = unit(read(mix_s, chunk))
            normed = (hat * param(2)).astype(bf16)
            normed = jnp.concatenate([normed, jnp.ones((LANES - channels, CHUNK), bf16)], axis=0)
            grad = grad_ref[0, :, pl.ds(at, CHUNK)]
            ex_s[...] = dot(we_ref[...], normed)
            dh_s[...] = dot(wrt_ref[...], (grad.astype(f32) * param(3)).astype(bf16))
            for h in range(0, hidden, 16):
                act, slope = gelu_both(ex_s[h : h + 16, :])
                hid_s[h : h + 16, :] = act.astype(bf16)
                de_s[h : h + 16, :] = (slope * dh_s[h : h + 16, :]).astype(bf16)
            reduced = dot(wr_ref[...], hid_s[...])
            feat_ref[0, :, pl.ds(at, CHUNK)] = (
                read(base_s, chunk) + param(3) * reduced
            ).astype(bf16)
            dwr_ref[...] += dot(grad, hid_s[...], ((1,), (1,)))
            dwe_ref[...] += dot(de_s[...], normed, ((1,), (1,)))
            dn = dot(wet_ref[...], de_s[...])
            dvec_ref[2] += fold(dn * hat)
            write(mix_s, chunk, unit_back(dn * param(2), hat, scale))

    @pl.when((phase == 1) & jnp.logical_not(live))
    def _():
        feat_ref[...] = jnp.zeros(feat_ref.shape, bf16)

    @pl.when((phase == 2) & (slot == 0))
    def _():
        @pl.loop(0, channels, unroll=4)
        def _(c):
            at = pl.multiple_of(c * rows, rows)
            grad = mix_s[PAD : PAD + pairs, pl.ds(at, rows), :]
            grad = grad.reshape(pairs * rows, LANES).astype(bf16)
            grad = dot(grad, mirror).astype(bf16)
            cross = dot(grad, gathered(base_s, c), ((0,), (0,)))
            for r in range(2):
                for k in range(BLOCKS // 2):
                    part = cross[r * SIDE : (r + 1) * SIDE, k * LANES : (k + 1) * LANES]
                    part = pltpu.roll(
                        jnp.where(near_mirrored, part, 0.0), 0, 1, stride=1, stride_axis=0
                    )
                    dk_ref[c, r * 5 + k : r * 5 + k + 1, :] = jnp.sum(
                        part, axis=0, keepdims=True
                    )
            out = dot(gathered(mix_s, c), toeplitz(back_ref, c))
            mix_s[PAD : PAD + pairs, pl.ds(at, rows), :] = out.reshape(pairs, rows, LANES)

    @pl.when((phase == 2) & live)
    def _():
        @pl.loop(0, chunks, unroll=2)
        def _(chunk):
            at = pl.multiple_of(chunk * CHUNK, CHUNK)
            pix = pix_ref[0, :, pl.ds(at, CHUNK)]
            hat, scale = unit(dot(ws_ref[...], pix))
            dbase = grad_ref[0, :, pl.ds(at, CHUNK)].astype(f32) + read(mix_s, chunk)
            dvec_ref[0] += fold(dbase * hat)
            dvec_ref[1] += fold(dbase)
            dstem = unit_back(dbase * param(0), hat, scale).astype(bf16)
            dws_ref[:, : pix.shape[0]] += dot(dstem, pix, ((1,), (1,)))

    @pl.when((phase == 2) & (slot == slots - 1))
    def _():
        mixed = dws_ref[...]
        for at in range(BLOCKS):
            mixed += lax.dot_general(
                dk_ref[:, at, :], pick_ref[at], (((1,), (0,)), ((), ())), precision=EXACT,
                preferred_element_type=f32,
            )
        products = dwr_ref[...]
        singles = [jnp.sum(dvec_ref[at], axis=1, keepdims=True) for at in range(3)]
        singles.append(jnp.sum(products * wr_ref[...].astype(f32), axis=1, keepdims=True))
        lane = lax.broadcasted_iota(jnp.int32, (channels, LANES), 1)
        start = first_single(pix_ref.shape[1])
        for at, single in enumerate(singles):
            mixed = jnp.where(lane == start + at, single, mixed)
        sums_ref[:channels] = mixed
        sums_ref[channels : channels + hidden] = dwe_ref[...]
        top = channels + hidden
        for at in range(hidden // LANES):
            sums_ref[top : top + channels] = products[:, at * LANES : (at + 1) * LANES] * par_ref[3]
            top += channels
        if top < sums_ref.shape[0]:
            sums_ref[top:] = jnp.zeros((sums_ref.shape[0] - top, LANES), f32)


def first_single(patch):
    return patch + KSIZE * KSIZE


def tap_places(patch):
    half = KSIZE // 2
    taps = KSIZE * KSIZE
    place = np.zeros((BLOCKS, taps, LANES), np.float32)
    pick = np.zeros((BLOCKS, LANES, LANES), np.float32)
    for m in range(BLOCKS):
        for r in range(2):
            a = m - 2 * PAD - r
            if abs(a) > half:
                continue
            for b in range(-half, half + 1):
                tap = (a + half) * KSIZE + b + half
                place[m, tap, (r * SIDE - b) % LANES] = 1.0
                k, rr = divmod(m, 2)
                pick[r * 5 + k, (rr * SIDE + b + SIDE - 1) % LANES, patch + tap] = 1.0
    return place, pick


def encode_slots(pixels, feature_grad, count, weights, share=1):
    (ws, stem_gain, stem_shift, kernel, block_gain, we, bias, wr, layer_scale) = weights
    slots, patch, area = pixels.shape
    channels = ws.shape[0]
    hidden = we.shape[0]
    pairs = area // LANES
    place, pick = tap_places(patch)
    total = channels + hidden + channels * (hidden // LANES)
    total = -(-total // (8 * share)) * 8 * share

    def pix_at(phase, slot, count):
        last = count[0] - 1
        return (jnp.where(phase == 1, last, jnp.minimum(slot, last)), 0, 0)

    def grad_at(phase, slot, count):
        return (jnp.where(phase == 0, 0, jnp.minimum(slot, count[0] - 1)), 0, 0)

    def feat_at(phase, slot, count):
        return (jnp.where(phase == 0, 0, jnp.where(phase == 1, slot, slots - 1)), 0, 0)

    def whole(shape):
        return pl.BlockSpec(shape, lambda phase, slot, count: (0,) * len(shape))

    consts = (
        ws, stem_gain[None], stem_shift[None], block_gain[None], layer_scale[None], kernel, we,
        bias[None], wr, jnp.asarray(place, bf16), jnp.asarray(place[:, ::-1], bf16),
        jnp.asarray(pick),
    )
    return pl.pallas_call(
        body,
        grid_spec=pltpu.PrefetchScalarGridSpec(
            num_scalar_prefetch=1,
            grid=(3, slots),
            in_specs=[
                pl.BlockSpec((1, patch, area), pix_at),
                pl.BlockSpec((1, channels, area), grad_at),
            ]
            + [whole(item.shape) for item in consts],
            out_specs=[pl.BlockSpec((1, channels, area), feat_at), whole((total, LANES))],
            scratch_shapes=[
                pltpu.VMEM((pairs + 2 * PAD, channels * slots, LANES), f32),
                pltpu.VMEM((pairs + 2 * PAD, channels * slots, LANES), f32),
                pltpu.VMEM((hidden, CHUNK), f32),
                pltpu.VMEM((hidden, CHUNK), f32),
                pltpu.VMEM((hidden, CHUNK), bf16),
                pltpu.VMEM((hidden, CHUNK), bf16),
                pltpu.VMEM((4, channels, LANES), f32),
                pltpu.VMEM((hidden, LANES), bf16),
                pltpu.VMEM((channels, hidden), bf16),
                pltpu.VMEM((hidden, channels), bf16),
                pltpu.VMEM((channels, 16, LANES), f32),
                pltpu.VMEM((channels, 16, LANES), f32),
                pltpu.VMEM((channels, LANES), f32),
                pltpu.VMEM((3, channels, LANES), f32),
                pltpu.VMEM((hidden, LANES), f32),
                pltpu.VMEM((channels, hidden), f32),
                pltpu.VMEM((channels, 16, LANES), f32),
            ],
        ),
        out_shape=[
            jax.ShapeDtypeStruct((slots, channels, area), bf16),
            jax.ShapeDtypeStruct((total, LANES), f32),
        ],
        compiler_params=pltpu.CompilerParams(
            dimension_semantics=("arbitrary", "arbitrary"), vmem_limit_bytes=60 * 2**20
        ),
    )(count, pixels, feature_grad, *consts)


def add_up(
    sums_ref, stem_ref, gain_ref, shift_ref, kernel_ref, norm_ref, expand_ref, bias_ref, reduce_ref,
    scale_ref, land_e, land_r, part, middle, full, out_sems, in_sems,
):
    count_e = lax.axis_size("enc")
    count_r = lax.axis_size("region")
    me_e = lax.axis_index("enc")
    me_r = lax.axis_index("region")
    barrier = pltpu.get_barrier_semaphore()
    for d in range(1, count_e):
        pl.semaphore_signal(
            barrier, 1, device_id={"enc": lax.rem(me_e + d, count_e)}, device_id_type=MESH
        )
    for d in range(1, count_r):
        pl.semaphore_signal(
            barrier, 1, device_id={"region": lax.rem(me_r + d, count_r)}, device_id_type=MESH
        )
    pl.semaphore_wait(barrier, count_e + count_r - 2)
    size_e = part.shape[0]
    size_r = land_r.shape[1]
    sems = iter(range(2 * (count_e + count_r - 2)))

    def block(index, size):
        return pl.ds(pl.multiple_of(index * size, 8), size)

    def exchange(axis, count, me, source, target):
        copies = []
        for d in range(1, count):
            peer = lax.rem(me + d, count)
            sem = next(sems)
            copy = pltpu.make_async_remote_copy(
                src_ref=source(peer), dst_ref=target(d), send_sem=out_sems.at[sem],
                recv_sem=in_sems.at[sem], device_id={axis: peer}, device_id_type=MESH,
            )
            copy.start()
            copies.append(copy)
        for copy in copies:
            copy.wait()

    exchange(
        "enc", count_e, me_e, lambda peer: sums_ref.at[block(peer, size_e)],
        lambda d: land_e.at[d - 1],
    )
    value = sums_ref[block(me_e, size_e)]
    for d in range(1, count_e):
        value += land_e[d - 1]
    part[...] = value
    exchange(
        "region", count_r, me_r, lambda peer: part.at[block(peer, size_r)],
        lambda d: land_r.at[d - 1],
    )
    value = part[block(me_r, size_r)]
    for d in range(1, count_r):
        value += land_r[d - 1]
    middle[block(me_r, size_r)] = value
    mine = middle.at[block(me_r, size_r)]
    exchange("region", count_r, me_r, lambda peer: mine, lambda d: mine)
    full[block(me_e, size_e)] = middle[...]
    own = full.at[block(me_e, size_e)]
    exchange("enc", count_e, me_e, lambda peer: own, lambda d: own)

    channels, patch = stem_ref.shape
    hidden = expand_ref.shape[0]
    mixed = full[:channels]
    stem_ref[...] = mixed[:, :patch]
    start = first_single(patch)
    kernel_ref[...] = mixed[:, patch:start]
    turned = jnp.transpose(mixed)
    for at, ref in enumerate((gain_ref, shift_ref, norm_ref, scale_ref)):
        ref[...] = turned[start + at : start + at + 1]
    wide_rows = full[channels : channels + hidden]
    expand_ref[...] = wide_rows[:, :channels]
    bias_ref[...] = jnp.transpose(wide_rows)[channels : channels + 1]
    top = channels + hidden
    for at in range(hidden // LANES):
        reduce_ref[:, at * LANES : (at + 1) * LANES] = full[top : top + channels]
        top += channels


def summed_over_devices(sums, weights):
    count_e = lax.axis_size("enc")
    count_r = lax.axis_size("region")
    size_e = sums.shape[0] // count_e
    size_r = size_e // count_r
    copies = 2 * (count_e + count_r - 2)
    shapes = [item.shape if item.ndim == 2 else (1, item.shape[0]) for item in weights]
    outs = pl.pallas_call(
        add_up,
        in_specs=[pl.BlockSpec(memory_space=pltpu.VMEM)],
        out_specs=[pl.BlockSpec(memory_space=pltpu.VMEM)] * len(shapes),
        out_shape=[jax.ShapeDtypeStruct(shape, f32) for shape in shapes],
        scratch_shapes=[
            pltpu.VMEM((count_e - 1, size_e, LANES), f32),
            pltpu.VMEM((count_r - 1, size_r, LANES), f32),
            pltpu.VMEM((size_e, LANES), f32),
            pltpu.VMEM((size_e, LANES), f32),
            pltpu.VMEM(sums.shape, f32),
            pltpu.SemaphoreType.DMA((copies,)),
            pltpu.SemaphoreType.DMA((copies,)),
        ],
        compiler_params=pltpu.CompilerParams(collective_id=0, has_side_effects=True),
    )(sums)
    return tuple(out.reshape(item.shape) for out, item in zip(outs, weights))


def on_device(pixels, feature_grad, tissue_count, *weights):
    share = lax.axis_size("enc") * lax.axis_size("region")
    features, sums = encode_slots(pixels, feature_grad, tissue_count, weights, share)
    return (features, *summed_over_devices(sums, weights))


def solution(mesh):
    return jax.shard_map(
        on_device,
        mesh=mesh,
        in_specs=(
            P(("region", "enc"), None, None),
            P(("region", "enc"), None, None),
            P(("region", "enc")),
        )
        + (P(),) * 9,
        out_specs=(P(("region", "enc"), None, None),) + (P(),) * 9,
        check_vma=False,
    )
```
